32 devices in a mesh: groups: 2 (over x), wide: 16 (over z, y, core).
Axes of the slice: x: 2, y: 2, z: 4, core: 2. Of those that a mesh axis runs over, the one named last changes fastest.
Arguments:
- tile_counts: int32 [32], P('groups'), parts along dimension 0, may hold values from 1 to 4
- text_lengths: int32 [32], P('groups'), parts along dimension 0, may hold values from 1 to 4
- page_table: int32 [32], P('groups'), parts along dimension 0, may hold values from 0 to 15, each once
- patches: bfloat16 [128, 4, 1176], P(('groups', 'wide')), parts along dimension 0, may hold values from -6 to 6
- patch_weight: bfloat16 [1176, 1280], replicated, may hold values from -0.1875 to 0.1875
- vision_gain: float32 [1280], replicated, may hold values from 0.1 to 1.9
- merger_inner: bfloat16 [5120, 5120], P(None, 'wide'), may hold values from -0.078125 to 0.078125
- merger_weight: bfloat16 [5120, 8192], P(None, 'wide'), may hold values from -0.078125 to 0.078125
- text_embed: bfloat16 [256, 8192], P('groups', 'wide'), parts along dimension 0
- attn_gain: float32 [8192], replicated, may hold values from 0.1 to 1.9
- q_weight: bfloat16 [8192, 2048], P(None, 'wide')
- kv_weight: bfloat16 [8192, 512], P(None, 'wide')
- out_weight: bfloat16 [2048, 8192], P('wide'), may hold values from -0.25 to 0.25
Outputs:
- hidden: bfloat16 [256, 8192], P(('groups', 'wide')), parts along dimension 0
- kv_pool: bfloat16 [32, 2, 2, 8, 128], P(('groups', 'wide')), parts along dimension 0
The draws below stay inside these ranges and needn't reach their ends.
There are 2 independent parts, one for each index of `groups`. The reference program is written for one: setup_inputs(seed, part) draws one part's arguments, and reference() takes and returns one part's arrays. A program takes and returns all parts, laid end to end along the dimension named above; an argument that names none is the same for every part. Nothing has to cross between parts.
Inputs may be any that keep to these rules, and one draw needn't show every extreme that they name: page_table names every page once.
All inputs are finite; a program needn't handle non-finite values.
Results may differ from the reference program's by a relative error of at most 0.007.
Values may be sent and summed in bfloat16 or wider, within the bound.
A program may use at most 128 MiB of HBM per device.

```python
import math
import jax
import jax.numpy as jnp
from jax import lax

PD = 1176
VD = 1280
MD = 5120
LD = 8192
HD = 128
TOK_DEV = 8
MAXT = 4
PAGE = 8
QHEADS = 16
KVH = 2
TOKENS = 128
BLOCKS = 16
N_WIDE = 16


def key_value_base(key):
    raw = jax.random.normal(jax.random.fold_in(key, 11), (LD, KVH * 2 * HD), jnp.float32)
    return jnp.clip(raw, -6.0, 6.0) * (1.0 / math.sqrt(LD))


def draw_kv_weight(key, part):
    return key_value_base(key).astype(jnp.bfloat16)


def draw_q_weight(key, part):
    raw = jax.random.normal(jax.random.fold_in(key, 13), (LD, QHEADS, HD), jnp.float32)
    drawn = jnp.clip(raw, -6.0, 6.0) * (1.0 / math.sqrt(LD))
    return drawn.reshape(LD, QHEADS * HD).astype(jnp.bfloat16)


def draw_text_embed(key, part):
    noise = jnp.clip(jax.random.normal(jax.random.fold_in(key, 19), (TOKENS, LD), jnp.float32), -6.0, 6.0)
    return noise.astype(jnp.bfloat16)


def place_ends(drawn, rng, least, top_value):
    longest = drawn.shape.index(max(drawn.shape))
    spots = []
    for shift in (0, 1):
        where = [jax.random.randint(jax.random.fold_in(rng, axis), (), 0, length) for axis, length in enumerate(drawn.shape)]
        where[longest] = (where[longest] + shift) % drawn.shape[longest]
        spots.append(tuple(where))
    return drawn.at[spots[0]].set(least).at[spots[1]].set(top_value)


def level_of(own_key, dims, shards, least, top_value):
    def one(axis_at, blocks):
        steps = jax.random.uniform(jax.random.fold_in(jax.random.fold_in(own_key, 6), axis_at), (blocks,), jnp.float32, least / len(shards), top_value / len(shards))
        return jnp.repeat(jnp.exp(steps), dims[axis_at] // blocks).reshape((-1,) + (1,) * (len(dims) - axis_at - 1))

    factor_of = one(*shards[0])
    for cut in shards[1:]:
        factor_of = factor_of * one(*cut)
    return factor_of


def scatter_about(key, shape, spread, reach, pieces=(), held_as=jnp.bfloat16):
    array = spread * jax.random.normal(key, shape, jnp.float32)
    if pieces:
        array = array * level_of(key, shape, pieces, -0.22, 0.18)
    return jnp.clip(array, -reach, reach).astype(held_as)


def setup_inputs(seed: int = 0, part: int = 0) -> dict:
    streams_of = jax.random.split(jax.random.key(seed), 14)
    own_keys = jax.random.split(jax.random.fold_in(streams_of[13], part), 14)
    return {
        "tile_counts": place_ends(jax.random.randint(own_keys[0], (N_WIDE,), 1, MAXT + 1), jax.random.fold_in(own_keys[0], 1), 1, MAXT).astype(jnp.int32),
        "text_lengths": place_ends(jax.random.randint(own_keys[1], (N_WIDE,), 1, TOK_DEV - MAXT + 1), jax.random.fold_in(own_keys[1], 1), 1, TOK_DEV - MAXT).astype(jnp.int32),
        "page_table": jax.random.permutation(own_keys[2], BLOCKS).astype(jnp.int32),
        "patches": scatter_about(own_keys[3], (N_WIDE * MAXT, 4, PD), 1.0, 6.0, ((0, 16),)),
        "patch_weight": scatter_about(streams_of[4], (PD, VD), PD ** -0.5, 0.1875),
        "vision_gain": jnp.clip(1.0 + 0.18 * jax.random.normal(streams_of[5], (VD,), jnp.float32), 0.1, 1.9),
        "merger_inner": scatter_about(streams_of[6], (MD, MD), MD ** -0.5, 0.078125, ((1, 16),)),
        "merger_weight": scatter_about(streams_of[7], (MD, LD), MD ** -0.5, 0.078125, ((1, 16),)),
        "text_embed": draw_text_embed(jax.random.fold_in(jax.random.fold_in(streams_of[13], part), 71), part),
        "attn_gain": jnp.clip(1.0 + 0.18 * jax.random.normal(streams_of[9], (LD,), jnp.float32), 0.1, 1.9),
        "q_weight": draw_q_weight(jax.random.fold_in(streams_of[13], 71), part),
        "kv_weight": draw_kv_weight(jax.random.fold_in(streams_of[13], 71), part),
        "out_weight": scatter_about(streams_of[12], (QHEADS * HD, LD), (HD * 4) ** -0.5, 0.25, ((0, 16),)),
    }


def encode_tiles(tiles, patch_weight, vision_gain):
    count = tiles.shape[0]
    flat = tiles.reshape(count * tiles.shape[1], tiles.shape[2])
    embedded = jnp.dot(flat, patch_weight, preferred_element_type=jnp.float32)
    mean_val = lax.optimization_barrier(jnp.mean(embedded, axis=1, keepdims=True))
    centred = embedded - mean_val
    variance = lax.optimization_barrier(jnp.mean(centred * centred, axis=1, keepdims=True))
    normed = centred * lax.rsqrt(variance + 1e-06) * vision_gain
    return normed.reshape(count, -1).astype(jnp.bfloat16)

def token_layout(tile_counts, text_lengths, homes, tok_dev, max_tiles):
    position = jnp.arange(homes * tok_dev, dtype=jnp.int32)
    owner = position // tok_dev
    offset = position % tok_dev
    tiles_here = tile_counts[owner]
    live = offset < tiles_here + text_lengths[owner]
    is_vision = offset < tiles_here
    vision_row = owner * max_tiles + jnp.minimum(offset, max_tiles - 1)
    segment = jnp.where(live, owner, homes + position)
    return (is_vision, vision_row.astype(jnp.int32), segment.astype(jnp.int32))

def attend_head(queries, keys, values, segment):
    position = jnp.arange(segment.shape[0], dtype=jnp.int32)
    scores = jnp.dot(queries, keys.T, preferred_element_type=jnp.float32) * (1.0 / math.sqrt(queries.shape[1]))
    allowed = (segment[:, None] == segment[None, :]) & (position[None, :] <= position[:, None])
    scores = jnp.where(allowed, scores, jnp.float32(-1e+30))
    highest = lax.optimization_barrier(jnp.max(scores, axis=1, keepdims=True))
    weights = jnp.exp(scores - highest)
    probs = (weights / lax.optimization_barrier(jnp.sum(weights, axis=1, keepdims=True))).astype(jnp.bfloat16)
    return jnp.dot(probs, values, preferred_element_type=jnp.float32).astype(jnp.bfloat16)

def reference(tile_counts, text_lengths, page_table, patches, patch_weight, vision_gain, merger_inner, merger_weight, text_embed, attn_gain, q_weight, kv_weight, out_weight):
    vision_hidden = encode_tiles(patches, patch_weight, vision_gain)
    lifted = jnp.dot(vision_hidden, merger_inner, preferred_element_type=jnp.float32)
    merger_act = jax.nn.gelu(lifted, approximate=False).astype(jnp.bfloat16)
    vision_embed = jnp.dot(merger_act, merger_weight, preferred_element_type=jnp.float32).astype(jnp.bfloat16)
    is_vision, vision_row, segment = token_layout(tile_counts, text_lengths, N_WIDE, TOK_DEV, MAXT)
    inputs = jnp.where(is_vision[:, None], jnp.take(vision_embed, vision_row, axis=0), text_embed)
    inputs_f = inputs.astype(jnp.float32)
    mean_sq = lax.optimization_barrier(jnp.mean(inputs_f * inputs_f, axis=1))
    normed = (inputs_f * lax.rsqrt(mean_sq + 1e-06)[:, None] * attn_gain).astype(jnp.bfloat16)
    queries = jnp.dot(normed, q_weight, preferred_element_type=jnp.float32).astype(jnp.bfloat16)
    keyvals = jnp.dot(normed, kv_weight, preferred_element_type=jnp.float32).astype(jnp.bfloat16)

    def one_head(head):
        group = head // 8
        query_cols = lax.dynamic_slice_in_dim(queries, head * HD, HD, 1)
        key_cols = lax.dynamic_slice_in_dim(keyvals, 2 * group * HD, HD, 1)
        value_cols = lax.dynamic_slice_in_dim(keyvals, (2 * group + 1) * HD, HD, 1)
        return attend_head(query_cols, key_cols, value_cols, segment)
    context = lax.map(one_head, jnp.arange(QHEADS, dtype=jnp.int32))
    context = context.transpose(1, 0, 2).reshape(TOKENS, QHEADS * HD)
    hidden = (inputs_f + jnp.dot(context, out_weight, preferred_element_type=jnp.float32)).astype(jnp.bfloat16)
    blocks = keyvals.reshape(BLOCKS, PAGE, KVH, 2, HD).transpose(0, 3, 2, 1, 4)
    kv_pool = jnp.zeros_like(blocks).at[page_table].set(blocks)
    return (hidden, kv_pool)
```

```python
import functools
import math

import jax
import jax.numpy as jnp
from jax import lax
from jax.experimental import pallas as pl
from jax.experimental.pallas import tpu as pltpu
from jax.sharding import PartitionSpec as P

HD = 128
TOK_DEV = 8
MAXT = 4
PAGE = 8
CHUNKS = 4
MESH = pl.DeviceIdType.MESH
F32 = jnp.float32
BF16 = jnp.bfloat16


def mm(a, b):
    return jnp.dot(a, b, preferred_element_type=F32)


def mm_t(a, b):
    return lax.dot_general(a, b, (((1,), (1,)), ((), ())), preferred_element_type=F32)


def iota(shape, dim):
    return lax.broadcasted_iota(jnp.int32, shape, dim)


def one_hot(condition):
    return jnp.where(condition, 1.0, 0.0).astype(BF16)


def slot_of(row, low_rows):
    high = row >= low_rows
    inner = jnp.where(high, row - low_rows, row)
    return (inner // MAXT) * TOK_DEV + inner % MAXT + jnp.where(high, MAXT, 0)


class Gather:
    def __init__(self, n, land, send, recv):
        me = lax.axis_index("wide")
        self.n, self.land, self.send, self.recv = n, land, send, recv
        self.depth = n // 4
        self.core, self.y, self.z = me % 2, (me // 2) % 2, me // 4
        self.me = me
        self.y_partner = self.index(self.z, 1 - self.y, self.core)
        self.sibling = self.index(self.z, self.y, 1 - self.core)

    def index(self, z, y, core):
        return z * 4 + y * 2 + core

    def copy(self, block, slot, target):
        return pltpu.make_async_remote_copy(
            src_ref=self.land.at[block],
            dst_ref=self.land.at[block],
            send_sem=self.send.at[slot],
            recv_sem=self.recv.at[block],
            device_id={"wide": target},
            device_id_type=MESH,
        )

    def arrived(self, block):
        self.copy(block, 0, self.sibling).wait_recv()

    def start(self):
        depth = self.depth

        def along(step, carry):
            peer = self.index((self.z + step) % depth, self.y, self.core)
            self.copy(self.me, step - 1, peer).start()
            return carry

        lax.fori_loop(1, depth, along, 0)
        self.copy(self.me, depth - 1, self.y_partner).start()
        self.copy(self.me, depth, self.sibling).start()

    def z_phase(self, use=None):
        depth = self.depth
        if use is not None:
            use(self.me)

        def step_of(step, carry):
            block = self.index((self.z + depth - step) % depth, self.y, self.core)
            self.arrived(block)
            self.copy(block, depth + step, self.y_partner).start()
            self.copy(block, 2 * depth - 1 + step, self.sibling).start()
            if use is not None:
                use(block)
            return carry

        lax.fori_loop(1, depth, step_of, 0)

    def y_phase(self, use=None):
        depth = self.depth

        def step_of(step, carry):
            block = self.index((self.z + depth - step) % depth, 1 - self.y, self.core)
            self.arrived(block)
            self.copy(block, 3 * depth - 1 + step, self.sibling).start()
            if use is not None:
                use(block)
            return carry

        lax.fori_loop(0, depth, step_of, 0)

    def core_phase(self, use=None):
        depth = self.depth
        for side in (self.y, 1 - self.y):

            def step_of(step, carry, side=side):
                block = self.index((self.z + depth - step) % depth, side, 1 - self.core)
                self.arrived(block)
                if use is not None:
                    use(block)
                return carry

            lax.fori_loop(0, depth, step_of, 0)

    def finish(self):
        def one(slot, carry):
            self.copy(self.me, slot, self.sibling).wait_send()
            return carry

        lax.fori_loop(0, self.n - 1, one, 0)


def layer_kernel(
    n,
    tiles_ref,
    lengths_ref,
    pages_ref,
    patches_ref,
    vgain_ref,
    text_ref,
    again_ref,
    pw_hbm,
    mi_hbm,
    mw_hbm,
    wq_hbm,
    wkv_hbm,
    ow_hbm,
    hidden_ref,
    pool_ref,
    pw,
    mi,
    mw,
    wq,
    wkv,
    ow,
    v_land,
    a_land,
    lo_land,
    hi_land,
    kv_land,
    vacc,
    qacc,
    kvacc,
    sqacc,
    ctx,
    home,
    part,
    ybuf,
    zsend,
    zbuf,
    own,
    fsend,
    frecv,
    w_sem,
    v_s,
    v_r,
    a_s,
    a_r,
    lo_s,
    lo_r,
    hi_s,
    hi_r,
    kv_s,
    kv_r,
    pair_s,
    pair_r,
    y_s,
    y_r,
    z_s,
    z_r,
    f_s,
    f_r,
):
    depth = n // 4
    me = lax.axis_index("wide")
    core, yy, zz = me % 2, (me // 2) % 2, me // 4
    low = n * MAXT
    slots = n * TOK_DEV
    width = text_ref.shape[1]
    inner = mi.shape[0]
    total_width = width * n
    half = total_width // 2
    cw = half // CHUNKS
    vis = vgain_ref.shape[1]

    gv = Gather(n, v_land, v_s, v_r)
    ga = Gather(n, a_land, a_s, a_r)
    glo = Gather(n, lo_land, lo_s, lo_r)
    ghi = Gather(n, hi_land, hi_s, hi_r)
    gkv = Gather(n, kv_land, kv_s, kv_r)
    y_partner, sibling = gv.y_partner, gv.sibling

    loads = [
        pltpu.make_async_copy(pw_hbm, pw, w_sem.at[0]),
        pltpu.make_async_copy(mi_hbm, mi, w_sem.at[1]),
        pltpu.make_async_copy(mw_hbm, mw, w_sem.at[2]),
        pltpu.make_async_copy(wq_hbm, wq, w_sem.at[3]),
        pltpu.make_async_copy(wkv_hbm, wkv, w_sem.at[4]),
        pltpu.make_async_copy(
            ow_hbm.at[:, pl.ds(pl.multiple_of(core * half, half), half)], ow.at[core], w_sem.at[5]
        ),
    ]
    for load in loads:
        load.start()

    barrier = pltpu.get_barrier_semaphore()

    def greet(step, carry):
        peer = ((zz + step) % depth) * 4 + yy * 2 + core
        pl.semaphore_signal(barrier, inc=1, device_id={"wide": peer}, device_id_type=MESH)
        return carry

    lax.fori_loop(1, depth, greet, 0)
    pl.semaphore_signal(barrier, inc=1, device_id={"wide": y_partner}, device_id_type=MESH)
    pl.semaphore_signal(barrier, inc=1, device_id={"wide": sibling}, device_id_type=MESH)

    loads[0].wait()
    embedded = mm(patches_ref[...], pw[...])
    centred = embedded - jnp.mean(embedded, axis=1, keepdims=True)
    variance = jnp.mean(centred * centred, axis=1, keepdims=True)
    v_land[me] = (centred * lax.rsqrt(variance + 1e-06) * vgain_ref[...]).astype(BF16)
    order = one_hot(slot_of(iota((slots, slots), 0), low) == iota((slots, slots), 1))
    text_rows = mm(order, text_ref[...])
    hi_land[me] = text_rows[low:].astype(BF16)

    pl.semaphore_wait(barrier, depth + 1)
    gv.start()
    ghi.start()
    ow_copy = pltpu.make_async_remote_copy(
        src_ref=ow_hbm.at[:, pl.ds(pl.multiple_of((1 - core) * half, half), half)],
        dst_ref=ow.at[core],
        send_sem=pair_s.at[0],
        recv_sem=pair_r.at[0],
        device_id={"wide": sibling},
        device_id_type=MESH,
    )
    gv.z_phase()
    gv.y_phase()
    gv.core_phase()

    loads[1].wait()
    every = v_land[...].reshape(n * 16, vis)
    tile_row, patch_row = iota((low, n * 16), 0), iota((low, n * 16), 1)
    lifted = jnp.zeros((low, inner), F32)
    for p in range(4):
        pick = one_hot(patch_row == tile_row * 4 + p)
        lifted = lifted + mm_t(mm(pick, every).astype(BF16), mi[:, p * vis : (p + 1) * vis])
    a_land[me] = (0.5 * lifted * (1.0 + lax.erf(lifted * math.sqrt(0.5)))).astype(BF16)
    ga.start()
    ghi.z_phase()

    loads[2].wait()
    vacc[...] = jnp.zeros_like(vacc)

    def merge(block):
        rows = pl.ds(pl.multiple_of(block * inner, 16), inner)
        vacc[...] += mm(a_land[block], mw[rows, :])

    ga.z_phase(merge)
    ga.y_phase(merge)
    ga.core_phase(merge)

    owner_low = iota((low, n), 0) // MAXT == iota((low, n), 1)
    tiles_low = jnp.sum(
        jnp.where(owner_low, tiles_ref[...].astype(F32), 0.0), axis=1, keepdims=True
    )
    is_vision = (iota((low, 1), 0) % MAXT).astype(F32) < tiles_low
    vision = vacc[...].astype(BF16).astype(F32)
    lo_land[me] = jnp.where(is_vision, vision, text_rows[:low]).astype(BF16)
    glo.start()
    ow_copy.start()

    loads[3].wait()
    loads[4].wait()
    qacc[...] = jnp.zeros_like(qacc)
    kvacc[...] = jnp.zeros_like(kvacc)
    sqacc[...] = jnp.zeros_like(sqacc)

    def project(which, land):
        def use(block):
            x = land[block].astype(F32)
            sqacc[which] += jnp.sum(x * x, axis=1, keepdims=True)
            scaled = (x * again_ref[block]).astype(BF16)
            span = pl.ds(pl.multiple_of(block * width, 128), width)
            qacc[which] += mm(scaled, wq[span, :])
            kvacc[which] += mm_t(wkv[:, span], scaled)

        return use

    ghi.y_phase(project(1, hi_land))
    glo.z_phase(project(0, lo_land))
    glo.y_phase(project(0, lo_land))
    ghi_use = project(1, hi_land)
    ghi_use(me)

    def behind(step, carry):
        ghi_use(((zz + depth - step) % depth) * 4 + yy * 2 + core)
        return carry

    lax.fori_loop(1, depth, behind, 0)
    ghi.core_phase(ghi_use)
    glo.core_phase(project(0, lo_land))

    queries = jnp.zeros((slots, HD), F32)
    keyvals = jnp.zeros((kvacc.shape[1], slots), F32)
    eye = iota((low, low), 0) == iota((low, low), 1)
    for which in range(2):
        scale = lax.rsqrt(sqacc[which] * (1.0 / total_width) + 1e-06)
        across = jnp.sum(jnp.where(eye, scale, 0.0), axis=0, keepdims=True)
        slot_col = slot_of(iota((low, slots), 0) + which * low, low)
        to_slot = one_hot(slot_col == iota((low, slots), 1))
        keyvals = keyvals + mm((kvacc[which] * across).astype(BF16), to_slot)
        slot_row = slot_of(iota((slots, low), 1) + which * low, low)
        from_slot = one_hot(slot_row == iota((slots, low), 0))
        queries = queries + mm(from_slot, (qacc[which] * scale).astype(BF16))
    kv_land[me] = keyvals.astype(BF16)
    gkv.start()
    queries = queries.astype(BF16)

    chip = me // 2
    wanted = chip * 16 + iota((16, low), 0)
    pick_lo = one_hot(slot_of(iota((16, low), 1), low) == wanted)
    pick_hi = one_hot(slot_of(iota((16, low), 1) + low, low) == wanted)

    def residual(step, carry):
        block = core * (n // 2) + step
        rows = mm(pick_lo, lo_land[block]) + mm(pick_hi, hi_land[block])
        home[:, pl.ds(pl.multiple_of(step * width, 128), width)] = rows
        return carry

    gkv.z_phase()
    gkv.y_phase()
    lax.fori_loop(0, n // 2, residual, 0)
    gkv.core_phase()

    group = me // 8
    keys_t = kv_land[pl.ds(group * 8, 4)].reshape(HD, slots)
    values_t = kv_land[pl.ds(group * 8 + 4, 4)].reshape(HD, slots)
    q_pos, k_pos = iota((slots, slots), 0), iota((slots, slots), 1)
    owner = iota((slots, n), 0) // TOK_DEV == iota((slots, n), 1)
    count_row = (tiles_ref[...] + lengths_ref[...]).astype(F32)
    count = jnp.sum(jnp.where(owner, count_row, 0.0), axis=1, keepdims=True)
    live = (iota((slots, 1), 0) % TOK_DEV).astype(F32) < count
    same = (q_pos // TOK_DEV == k_pos // TOK_DEV) & (k_pos <= q_pos)
    floor = jnp.float32(-1e30)
    scores = mm(queries, keys_t) * (1.0 / math.sqrt(HD))
    within = jnp.where(live, jnp.where(same, scores, floor), floor)
    scores = jnp.where(q_pos == k_pos, scores, within)
    weights = jnp.exp(scores - jnp.max(scores, axis=1, keepdims=True))
    probs = (weights / jnp.sum(weights, axis=1, keepdims=True)).astype(BF16)
    ctx[core] = mm_t(probs, values_t).astype(BF16)
    ctx_copy = pltpu.make_async_remote_copy(
        src_ref=ctx.at[core],
        dst_ref=ctx.at[core],
        send_sem=pair_s.at[1],
        recv_sem=pair_r.at[1],
        device_id={"wide": sibling},
        device_id_type=MESH,
    )
    ctx_copy.start()

    mine = jnp.where(pages_ref[...] == me, 1.0, 0.0)
    mine_rows = jnp.broadcast_to(mine, (PAGE, n)).astype(BF16)
    spread = one_hot(iota((n, slots), 0) == iota((n, slots), 1) // PAGE)
    in_page = iota((PAGE, slots), 1) % PAGE == iota((PAGE, slots), 0)
    chosen = jnp.where(in_page, mm(mine_rows, spread), 0.0).astype(BF16)
    for g in range(n // 8):
        for kind in range(2):
            first = g * 8 + kind * 4
            rows_t = kv_land[first : first + 4].reshape(HD, slots)
            pool_ref[0, kind, g] = mm_t(chosen, rows_t).astype(BF16)

    loads[5].wait()
    ow_copy.wait_recv()
    ctx_copy.wait_recv()

    both = jnp.concatenate([ctx[0], ctx[1]], axis=1)

    def y_copy(k):
        return pltpu.make_async_remote_copy(
            src_ref=part.at[k, 1 - yy],
            dst_ref=ybuf.at[k],
            send_sem=y_s.at[k],
            recv_sem=y_r.at[k],
            device_id={"wide": y_partner},
            device_id_type=MESH,
        )

    def z_copy(k, step):
        peer_z = (zz + step) % depth
        return pltpu.make_async_remote_copy(
            src_ref=zsend.at[k, peer_z],
            dst_ref=zbuf.at[k, step],
            send_sem=z_s.at[k, step],
            recv_sem=z_r.at[k, step],
            device_id={"wide": peer_z * 4 + yy * 2 + core},
            device_id_type=MESH,
        )

    def f_copy(k):
        return pltpu.make_async_remote_copy(
            src_ref=fsend.at[k],
            dst_ref=frecv.at[k],
            send_sem=f_s.at[k],
            recv_sem=f_r.at[k],
            device_id={"wide": sibling},
            device_id_type=MESH,
        )

    for k in range(CHUNKS):
        cols = slice(k * cw, (k + 1) * cw)
        share = mm(both, ow[:, :, cols].reshape(2 * HD, cw)).astype(BF16)
        for z in range(depth):
            for y in range(2):
                row = (z * 2 + y) * 16
                part[k, y, z] = share[row : row + 16]
        y_copy(k).start()
    for k in range(CHUNKS):
        y_copy(k).wait_recv()
        for step in range(1, depth):
            peer_z = (zz + step) % depth
            summed = part[k, yy, peer_z].astype(F32) + ybuf[k, peer_z].astype(F32)
            zsend[k, peer_z] = summed.astype(BF16)
            z_copy(k, step).start()
        own[k] = (
            part[k, yy, zz].astype(F32)
            + ybuf[k, zz].astype(F32)
            + home[:, k * cw : (k + 1) * cw]
        )
    is_first = core == 0
    for k in range(CHUNKS):
        rows = own[k]
        for step in range(1, depth):
            z_copy(k, step).wait_recv()
            rows = rows + zbuf[k, step].astype(F32)
        upper, lower = rows[:TOK_DEV], rows[TOK_DEV:]
        fsend[k] = jnp.where(is_first, lower, upper).astype(BF16)
        f_copy(k).start()
        kept = jnp.where(is_first, upper, lower).astype(BF16)
        hidden_ref[:, pl.ds(pl.multiple_of(core * half + k * cw, 128), cw)] = kept
    for k in range(CHUNKS):
        f_copy(k).wait_recv()
        hidden_ref[:, pl.ds(pl.multiple_of((1 - core) * half + k * cw, 128), cw)] = frecv[k]

    ow_copy.wait_send()
    ctx_copy.wait_send()
    for k in range(CHUNKS):
        y_copy(k).wait_send()
        f_copy(k).wait_send()
        for step in range(1, depth):
            z_copy(k, step).wait_send()
    for gather in (gv, ga, glo, ghi, gkv):
        gather.finish()


def on_device(
    tile_counts,
    text_lengths,
    page_table,
    patches,
    patch_weight,
    vision_gain,
    merger_inner,
    merger_weight,
    text_embed,
    attn_gain,
    q_weight,
    kv_weight,
    out_weight,
):
    n = lax.axis_size("wide")
    depth = n // 4
    slots = n * TOK_DEV
    low = n * MAXT
    width = text_embed.shape[1]
    inner = merger_inner.shape[1]
    total_width = width * n
    half = total_width // 2
    cw = half // CHUNKS
    kv_cols = kv_weight.shape[1]
    vis = patch_weight.shape[1]
    dma = pltpu.SemaphoreType.DMA
    in_vmem = pl.BlockSpec(memory_space=pltpu.VMEM)
    in_any = pl.BlockSpec(memory_space=pl.ANY)
    scratch = [
        pltpu.VMEM(patch_weight.shape, BF16),
        pltpu.VMEM((inner, merger_inner.shape[0]), BF16),
        pltpu.VMEM(merger_weight.shape, BF16),
        pltpu.VMEM(q_weight.shape, BF16),
        pltpu.VMEM((kv_cols, total_width), BF16),
        pltpu.VMEM((2, HD, half), BF16),
        pltpu.VMEM((n, 16, vis), BF16),
        pltpu.VMEM((n, low, inner), BF16),
        pltpu.VMEM((n, low, width), BF16),
        pltpu.VMEM((n, low, width), BF16),
        pltpu.VMEM((n, kv_cols, slots), BF16),
        pltpu.VMEM((low, width), F32),
        pltpu.VMEM((2, low, HD), F32),
        pltpu.VMEM((2, kv_cols, low), F32),
        pltpu.VMEM((2, low, 1), F32),
        pltpu.VMEM((2, slots, HD), BF16),
        pltpu.VMEM((16, half), F32),
        pltpu.VMEM((CHUNKS, 2, depth, 16, cw), BF16),
        pltpu.VMEM((CHUNKS, depth, 16, cw), BF16),
        pltpu.VMEM((CHUNKS, depth, 16, cw), BF16),
        pltpu.VMEM((CHUNKS, depth, 16, cw), BF16),
        pltpu.VMEM((CHUNKS, 16, cw), F32),
        pltpu.VMEM((CHUNKS, TOK_DEV, cw), BF16),
        pltpu.VMEM((CHUNKS, TOK_DEV, cw), BF16),
        dma((6,)),
    ]
    for _ in range(5):
        scratch += [dma((n,)), dma((n,))]
    scratch += [dma((2,)), dma((2,)), dma((CHUNKS,)), dma((CHUNKS,))]
    scratch += [dma((CHUNKS, depth)), dma((CHUNKS, depth)), dma((CHUNKS,)), dma((CHUNKS,))]
    hidden, pool = pl.pallas_call(
        functools.partial(layer_kernel, n),
        out_shape=(
            jax.ShapeDtypeStruct((TOK_DEV, total_width), BF16),
            jax.ShapeDtypeStruct((1, 2, n // 8, PAGE, HD), BF16),
        ),
        in_specs=[in_vmem] * 7 + [in_any] * 6,
        out_specs=(in_vmem, in_vmem),
        scratch_shapes=scratch,
        compiler_params=pltpu.CompilerParams(
            collective_id=0, has_side_effects=True, vmem_limit_bytes=56 * 2**20
        ),
        name="vision_prefill_layer",
    )(
        tile_counts.reshape(1, n),
        text_lengths.reshape(1, n),
        page_table.reshape(1, n),
        patches.reshape(-1, patches.shape[2]),
        vision_gain.reshape(1, -1),
        text_embed,
        attn_gain.reshape(n, 1, width),
        patch_weight,
        merger_inner.T,
        merger_weight,
        q_weight,
        kv_weight.T,
        out_weight,
    )
    return hidden, pool


def solution(mesh):
    in_specs = (
        P("groups"),
        P("groups"),
        P("groups"),
        P(("groups", "wide"), None, None),
        P(),
        P(),
        P(None, "wide"),
        P(None, "wide"),
        P("groups", "wide"),
        P(),
        P(None, "wide"),
        P(None, "wide"),
        P("wide", None),
    )
    out_specs = (P(("groups", "wide"), None), P(("groups", "wide"), None, None, None, None))
    return jax.shard_map(
        on_device, mesh=mesh, in_specs=in_specs, out_specs=out_specs, check_vma=False
    )
```

```python
import functools
import math

import jax
import jax.numpy as jnp
from jax import lax
from jax.experimental import pallas as pl
from jax.experimental.pallas import tpu as pltpu
from jax.sharding import PartitionSpec as P

HD = 128
TOK_DEV = 8
MAXT = 4
PAGE = 8
CHUNKS = 8
MESH = pl.DeviceIdType.MESH
F32 = jnp.float32
BF16 = jnp.bfloat16


def mm(a, b):
    return jnp.dot(a, b, preferred_element_type=F32)


def mm_t(a, b):
    return lax.dot_general(a, b, (((1,), (1,)), ((), ())), preferred_element_type=F32)


def iota(shape, dim):
    return lax.broadcasted_iota(jnp.int32, shape, dim)


def one_hot(condition):
    return jnp.where(condition, 1.0, 0.0).astype(BF16)


def slot_of(row, low_rows):
    high = row >= low_rows
    inner = jnp.where(high, row - low_rows, row)
    return (inner // MAXT) * TOK_DEV + inner % MAXT + jnp.where(high, MAXT, 0)


class Gather:
    def __init__(self, n, land, send, recv):
        me = lax.axis_index("wide")
        self.n, self.land, self.send, self.recv = n, land, send, recv
        self.depth = n // 4
        self.core, self.y, self.z = me % 2, (me // 2) % 2, me // 4
        self.me = me
        self.y_partner = self.index(self.z, 1 - self.y, self.core)
        self.sibling = self.index(self.z, self.y, 1 - self.core)

    def index(self, z, y, core):
        return z * 4 + y * 2 + core

    def copy(self, block, slot, target):
        return pltpu.make_async_remote_copy(
            src_ref=self.land.at[block],
            dst_ref=self.land.at[block],
            send_sem=self.send.at[slot],
            recv_sem=self.recv.at[block],
            device_id={"wide": target},
            device_id_type=MESH,
        )

    def arrived(self, block):
        self.copy(block, 0, self.sibling).wait_recv()

    def start(self):
        depth = self.depth

        def along(step, carry):
            peer = self.index((self.z + step) % depth, self.y, self.core)
            self.copy(self.me, step - 1, peer).start()
            return carry

        lax.fori_loop(1, depth, along, 0)
        self.copy(self.me, depth - 1, self.y_partner).start()
        self.copy(self.me, depth, self.sibling).start()

    def z_phase(self, use=None):
        depth = self.depth
        if use is not None:
            use(self.me)

        def step_of(step, carry):
            block = self.index((self.z + depth - step) % depth, self.y, self.core)
            self.arrived(block)
            self.copy(block, depth + step, self.y_partner).start()
            self.copy(block, 2 * depth - 1 + step, self.sibling).start()
            if use is not None:
                use(block)
            return carry

        lax.fori_loop(1, depth, step_of, 0)

    def y_phase(self, use=None):
        depth = self.depth

        def step_of(step, carry):
            block = self.index((self.z + depth - step) % depth, 1 - self.y, self.core)
            self.arrived(block)
            self.copy(block, 3 * depth - 1 + step, self.sibling).start()
            if use is not None:
                use(block)
            return carry

        lax.fori_loop(0, depth, step_of, 0)

    def core_phase(self, use=None):
        depth = self.depth
        for side in (self.y, 1 - self.y):

            def step_of(step, carry, side=side):
                block = self.index((self.z + depth - step) % depth, side, 1 - self.core)
                self.arrived(block)
                if use is not None:
                    use(block)
                return carry

            lax.fori_loop(0, depth, step_of, 0)

    def finish(self):
        def one(slot, carry):
            self.copy(self.me, slot, self.sibling).wait_send()
            return carry

        lax.fori_loop(0, self.n - 1, one, 0)


class GroupGather(Gather):
    def peer(self, step):
        return (self.me // 8) * 8 + (self.me + step) % 8

    def partner(self, step):
        groups = self.n // 8
        return ((self.me // 8 + step) % groups) * 8 + self.me % 8

    def spread(self, block, first):
        def one(step, carry):
            self.copy(block, first + step - 1, self.peer(step)).start()
            return carry

        lax.fori_loop(1, 8, one, 0)

    def start(self):
        self.spread(self.me, 0)
        for step in range(1, self.n // 8):
            self.copy(self.me, 6 + step, self.partner(step)).start()

    def wait_group(self):
        def one(step, carry):
            self.arrived(self.peer(step))
            return carry

        lax.fori_loop(1, 8, one, 0)

    def forward(self):
        groups = self.n // 8
        for step in range(1, groups):
            block = self.partner(step)
            self.arrived(block)
            self.spread(block, 6 + groups + (step - 1) * 7)

    def wait_others(self):
        groups = self.n // 8
        for step in range(1, groups):

            def one(i, carry, step=step):
                group = (self.me // 8 + step) % groups
                self.arrived(group * 8 + (self.me + i) % 8)
                return carry

            lax.fori_loop(1, 8, one, 0)


def layer_kernel(
    n,
    tiles_ref,
    lengths_ref,
    pages_ref,
    patches_ref,
    vgain_ref,
    text_ref,
    again_ref,
    pw_hbm,
    mi_hbm,
    mw_hbm,
    wq_hbm,
    wkv_hbm,
    ow_hbm,
    hidden_ref,
    pool_ref,
    pw,
    mi,
    mw,
    wq,
    wkv,
    ow,
    pixels,
    v_land,
    a_land,
    lo_land,
    hi_land,
    kv_land,
    vacc,
    qacc,
    kvacc,
    sqacc,
    ctx,
    home,
    part,
    ybuf,
    zsend,
    zbuf,
    own,
    fsend,
    frecv,
    w_sem,
    v_s,
    v_r,
    a_s,
    a_r,
    lo_s,
    lo_r,
    hi_s,
    hi_r,
    kv_s,
    kv_r,
    pair_s,
    pair_r,
    y_s,
    y_r,
    z_s,
    z_r,
    f_s,
    f_r,
):
    depth = n // 4
    me = lax.axis_index("wide")
    core, yy, zz = me % 2, (me // 2) % 2, me // 4
    low = n * MAXT
    slots = n * TOK_DEV
    width = text_ref.shape[1]
    inner = mi.shape[0]
    total_width = width * n
    half = total_width // 2
    cw = half // CHUNKS
    vis = vgain_ref.shape[0]

    gv = Gather(n, v_land, v_s, v_r)
    ga = Gather(n, a_land, a_s, a_r)
    glo = Gather(n, lo_land, lo_s, lo_r)
    ghi = Gather(n, hi_land, hi_s, hi_r)
    gkv = GroupGather(n, kv_land, kv_s, kv_r)
    y_partner, sibling = gv.y_partner, gv.sibling

    loads = [
        pltpu.make_async_copy(pw_hbm, pw, w_sem.at[0]),
        pltpu.make_async_copy(mi_hbm, mi, w_sem.at[1]),
        pltpu.make_async_copy(mw_hbm, mw, w_sem.at[2]),
        pltpu.make_async_copy(wq_hbm, wq, w_sem.at[3]),
        pltpu.make_async_copy(wkv_hbm, wkv, w_sem.at[4]),
        pltpu.make_async_copy(
            ow_hbm.at[:, pl.ds(pl.multiple_of(core * half, half), half)], ow.at[core], w_sem.at[5]
        ),
    ]
    loads[0].start()

    barrier = pltpu.get_barrier_semaphore()

    def greet(step, carry):
        peer = (me + step) % n
        pl.semaphore_signal(barrier, inc=1, device_id={"wide": peer}, device_id_type=MESH)
        return carry

    lax.fori_loop(1, n, greet, 0)

    for tile in range(patches_ref.shape[0]):
        pixels[tile * 4 : tile * 4 + 4] = patches_ref[tile].astype(F32)
    loads[0].wait()
    for load in loads[1:]:
        load.start()
    embedded = mm(pixels[...].astype(BF16), pw[...])
    centred = embedded - jnp.mean(embedded, axis=1, keepdims=True)
    variance = jnp.mean(centred * centred, axis=1, keepdims=True)
    v_land[me] = (centred * lax.rsqrt(variance + 1e-06) * vgain_ref[...].reshape(1, vis)).astype(BF16)
    order = one_hot(slot_of(iota((slots, slots), 0), low) == iota((slots, slots), 1))
    text_rows = mm(order, text_ref[...])
    hi_land[me] = text_rows[low:].astype(BF16)

    pl.semaphore_wait(barrier, n - 1)
    gv.start()
    ghi.start()
    ow_copy = pltpu.make_async_remote_copy(
        src_ref=ow_hbm.at[:, pl.ds(pl.multiple_of((1 - core) * half, half), half)],
        dst_ref=ow.at[core],
        send_sem=pair_s.at[0],
        recv_sem=pair_r.at[0],
        device_id={"wide": sibling},
        device_id_type=MESH,
    )
    gv.z_phase()
    gv.y_phase()
    gv.core_phase()
    ghi.z_phase()

    loads[1].wait()
    every = v_land[...].reshape(n * 16, vis)
    tile_row, patch_row = iota((low, n * 16), 0), iota((low, n * 16), 1)
    lifted = jnp.zeros((low, inner), F32)
    for p in range(4):
        pick = one_hot(patch_row == tile_row * 4 + p)
        lifted = lifted + mm_t(mm(pick, every).astype(BF16), mi[:, p * vis : (p + 1) * vis])
    a_land[me] = (0.5 * lifted * (1.0 + lax.erf(lifted * math.sqrt(0.5)))).astype(BF16)
    ga.start()

    loads[2].wait()
    vacc[...] = jnp.zeros_like(vacc)

    def merge(block):
        rows = pl.ds(pl.multiple_of(block * inner, 16), inner)
        vacc[...] += mm(a_land[block], mw[rows, :])

    ga.z_phase(merge)
    ga.y_phase(merge)
    ga.core_phase(merge)

    owner_low = iota((low, n), 0) // MAXT == iota((low, n), 1)
    tiles_low = jnp.sum(
        jnp.where(owner_low, tiles_ref[...].astype(F32), 0.0), axis=1, keepdims=True
    )
    is_vision = (iota((low, 1), 0) % MAXT).astype(F32) < tiles_low
    vision = vacc[...].astype(BF16).astype(F32)
    lo_land[me] = jnp.where(is_vision, vision, text_rows[:low]).astype(BF16)
    glo.start()
    ow_copy.start()

    loads[3].wait()
    loads[4].wait()
    qacc[...] = jnp.zeros_like(qacc)
    kvacc[...] = jnp.zeros_like(kvacc)
    sqacc[...] = jnp.zeros_like(sqacc)

    def project(which, land):
        def use(block):
            x = land[block].astype(F32)
            sqacc[which] += jnp.sum(x * x, axis=1, keepdims=True)
            scaled = (x * again_ref[block]).astype(BF16)
            span = pl.ds(pl.multiple_of(block * width, 128), width)
            qacc[which] += mm(scaled, wq[span, :])
            kvacc[which] += mm_t(wkv[:, span], scaled)

        return use

    ghi.y_phase(project(1, hi_land))
    glo.z_phase(project(0, lo_land))
    glo.y_phase(project(0, lo_land))
    ghi_use = project(1, hi_land)
    ghi_use(me)

    def behind(step, carry):
        ghi_use(((zz + depth - step) % depth) * 4 + yy * 2 + core)
        return carry

    lax.fori_loop(1, depth, behind, 0)
    ghi.core_phase(ghi_use)
    glo.core_phase(project(0, lo_land))

    queries = jnp.zeros((slots, HD), F32)
    keyvals = jnp.zeros((kvacc.shape[1], slots), F32)
    eye = iota((low, low), 0) == iota((low, low), 1)
    for which in range(2):
        scale = lax.rsqrt(sqacc[which] * (1.0 / total_width) + 1e-06)
        across = jnp.sum(jnp.where(eye, scale, 0.0), axis=0, keepdims=True)
        slot_col = slot_of(iota((low, slots), 0) + which * low, low)
        to_slot = one_hot(slot_col == iota((low, slots), 1))
        keyvals = keyvals + mm((kvacc[which] * across).astype(BF16), to_slot)
        slot_row = slot_of(iota((slots, low), 1) + which * low, low)
        from_slot = one_hot(slot_row == iota((slots, low), 0))
        queries = queries + mm(from_slot, (qacc[which] * scale).astype(BF16))
    kv_land[me] = keyvals.astype(BF16)
    gkv.start()
    queries = queries.astype(BF16)

    chip = me // 2
    wanted = chip * 16 + iota((16, low), 0)
    pick_lo = one_hot(slot_of(iota((16, low), 1), low) == wanted)
    pick_hi = one_hot(slot_of(iota((16, low), 1) + low, low) == wanted)

    def residual(step, carry):
        block = core * (n // 2) + step
        rows = mm(pick_lo, lo_land[block]) + mm(pick_hi, hi_land[block])
        home[:, pl.ds(pl.multiple_of(step * width, 128), width)] = rows
        return carry

    lax.fori_loop(0, n // 2, residual, 0)
    gkv.wait_group()

    group = me // 8
    keys_t = kv_land[pl.ds(group * 8, 4)].reshape(HD, slots)
    values_t = kv_land[pl.ds(group * 8 + 4, 4)].reshape(HD, slots)
    q_pos, k_pos = iota((slots, slots), 0), iota((slots, slots), 1)
    owner = iota((slots, n), 0) // TOK_DEV == iota((slots, n), 1)
    count_row = (tiles_ref[...] + lengths_ref[...]).astype(F32)
    count = jnp.sum(jnp.where(owner, count_row, 0.0), axis=1, keepdims=True)
    live = (iota((slots, 1), 0) % TOK_DEV).astype(F32) < count
    same = (q_pos // TOK_DEV == k_pos // TOK_DEV) & (k_pos <= q_pos)
    floor = jnp.float32(-1e30)
    scores = mm(queries, keys_t) * (1.0 / math.sqrt(HD))
    within = jnp.where(live, jnp.where(same, scores, floor), floor)
    scores = jnp.where(q_pos == k_pos, scores, within)
    weights = jnp.exp(scores - jnp.max(scores, axis=1, keepdims=True))
    probs = (weights / jnp.sum(weights, axis=1, keepdims=True)).astype(BF16)
    ctx[core] = mm_t(probs, values_t).astype(BF16)
    ctx_copy = pltpu.make_async_remote_copy(
        src_ref=ctx.at[core],
        dst_ref=ctx.at[core],
        send_sem=pair_s.at[1],
        recv_sem=pair_r.at[1],
        device_id={"wide": sibling},
        device_id_type=MESH,
    )
    ctx_copy.start()

    gkv.forward()

    loads[5].wait()
    ow_copy.wait_recv()
    ctx_copy.wait_recv()

    both = jnp.concatenate([ctx[0], ctx[1]], axis=1)

    def y_copy(k):
        return pltpu.make_async_remote_copy(
            src_ref=part.at[k, 1 - yy],
            dst_ref=ybuf.at[k],
            send_sem=y_s.at[k],
            recv_sem=y_r.at[k],
            device_id={"wide": y_partner},
            device_id_type=MESH,
        )

    def z_copy(k, step):
        peer_z = (zz + step) % depth
        return pltpu.make_async_remote_copy(
            src_ref=zsend.at[k, peer_z],
            dst_ref=zbuf.at[k, step],
            send_sem=z_s.at[k, step],
            recv_sem=z_r.at[k, step],
            device_id={"wide": peer_z * 4 + yy * 2 + core},
            device_id_type=MESH,
        )

    def f_copy(k):
        return pltpu.make_async_remote_copy(
            src_ref=fsend.at[k],
            dst_ref=frecv.at[k],
            send_sem=f_s.at[k],
            recv_sem=f_r.at[k],
            device_id={"wide": sibling},
            device_id_type=MESH,
        )

    for k in range(CHUNKS):
        cols = slice(k * cw, (k + 1) * cw)
        share = mm(both, ow[:, :, cols].reshape(2 * HD, cw)).astype(BF16)
        for z in range(depth):
            for y in range(2):
                row = (z * 2 + y) * 16
                part[k, y, z] = share[row : row + 16]
        y_copy(k).start()

    gkv.wait_others()
    mine = jnp.where(pages_ref[...] == me, 1.0, 0.0)
    mine_rows = jnp.broadcast_to(mine, (PAGE, n)).astype(BF16)
    spread = one_hot(iota((n, slots), 0) == iota((n, slots), 1) // PAGE)
    in_page = iota((PAGE, slots), 1) % PAGE == iota((PAGE, slots), 0)
    chosen = jnp.where(in_page, mm(mine_rows, spread), 0.0).astype(BF16)
    for g in range(n // 8):
        for kind in range(2):
            first = g * 8 + kind * 4
            rows_t = kv_land[first : first + 4].reshape(HD, slots)
            pool_ref[0, kind, g] = mm_t(chosen, rows_t).astype(BF16)

    for k in range(CHUNKS):
        y_copy(k).wait_recv()
        for step in range(1, depth):
            peer_z = (zz + step) % depth
            summed = part[k, yy, peer_z].astype(F32) + ybuf[k, peer_z].astype(F32)
            zsend[k, peer_z] = summed.astype(BF16)
            z_copy(k, step).start()
        own[k] = (
            part[k, yy, zz].astype(F32)
            + ybuf[k, zz].astype(F32)
            + home[:, k * cw : (k + 1) * cw]
        )
    is_first = core == 0
    for k in range(CHUNKS):
        rows = own[k]
        for step in range(1, depth):
            z_copy(k, step).wait_recv()
            rows = rows + zbuf[k, step].astype(F32)
        upper, lower = rows[:TOK_DEV], rows[TOK_DEV:]
        fsend[k] = jnp.where(is_first, lower, upper).astype(BF16)
        f_copy(k).start()
        kept = jnp.where(is_first, upper, lower).astype(BF16)
        hidden_ref[:, pl.ds(pl.multiple_of(core * half + k * cw, 128), cw)] = kept
    for k in range(CHUNKS):
        f_copy(k).wait_recv()
        hidden_ref[:, pl.ds(pl.multiple_of((1 - core) * half + k * cw, 128), cw)] = frecv[k]

    ow_copy.wait_send()
    ctx_copy.wait_send()
    for k in range(CHUNKS):
        y_copy(k).wait_send()
        f_copy(k).wait_send()
        for step in range(1, depth):
            z_copy(k, step).wait_send()
    for gather in (gv, ga, glo, ghi, gkv):
        gather.finish()


def on_device(
    tile_counts,
    text_lengths,
    page_table,
    patches,
    patch_weight,
    vision_gain,
    merger_inner,
    merger_weight,
    text_embed,
    attn_gain,
    q_weight,
    kv_weight,
    out_weight,
):
    n = lax.axis_size("wide")
    depth = n // 4
    slots = n * TOK_DEV
    low = n * MAXT
    width = text_embed.shape[1]
    inner = merger_inner.shape[1]
    total_width = width * n
    half = total_width // 2
    cw = half // CHUNKS
    kv_cols = kv_weight.shape[1]
    vis = patch_weight.shape[1]
    dma = pltpu.SemaphoreType.DMA
    in_vmem = pl.BlockSpec(memory_space=pltpu.VMEM)
    in_any = pl.BlockSpec(memory_space=pl.ANY)
    scratch = [
        pltpu.VMEM(patch_weight.shape, BF16),
        pltpu.VMEM((inner, merger_inner.shape[0]), BF16),
        pltpu.VMEM(merger_weight.shape, BF16),
        pltpu.VMEM(q_weight.shape, BF16),
        pltpu.VMEM((kv_cols, total_width), BF16),
        pltpu.VMEM((2, HD, half), BF16),
        pltpu.VMEM((16, patch_weight.shape[0]), F32),
        pltpu.VMEM((n, 16, vis), BF16),
        pltpu.VMEM((n, low, inner), BF16),
        pltpu.VMEM((n, low, width), BF16),
        pltpu.VMEM((n, low, width), BF16),
        pltpu.VMEM((n, kv_cols, slots), BF16),
        pltpu.VMEM((low, width), F32),
        pltpu.VMEM((2, low, HD), F32),
        pltpu.VMEM((2, kv_cols, low), F32),
        pltpu.VMEM((2, low, 1), F32),
        pltpu.VMEM((2, slots, HD), BF16),
        pltpu.VMEM((16, half), F32),
        pltpu.VMEM((CHUNKS, 2, depth, 16, cw), BF16),
        pltpu.VMEM((CHUNKS, depth, 16, cw), BF16),
        pltpu.VMEM((CHUNKS, depth, 16, cw), BF16),
        pltpu.VMEM((CHUNKS, depth, 16, cw), BF16),
        pltpu.VMEM((CHUNKS, 16, cw), F32),
        pltpu.VMEM((CHUNKS, TOK_DEV, cw), BF16),
        pltpu.VMEM((CHUNKS, TOK_DEV, cw), BF16),
        dma((6,)),
    ]
    for _ in range(5):
        scratch += [dma((n,)), dma((n,))]
    scratch += [dma((2,)), dma((2,)), dma((CHUNKS,)), dma((CHUNKS,))]
    scratch += [dma((CHUNKS, depth)), dma((CHUNKS, depth)), dma((CHUNKS,)), dma((CHUNKS,))]
    hidden, pool = pl.pallas_call(
        functools.partial(layer_kernel, n),
        out_shape=(
            jax.ShapeDtypeStruct((TOK_DEV, total_width), BF16),
            jax.ShapeDtypeStruct((1, 2, n // 8, PAGE, HD), BF16),
        ),
        in_specs=[in_vmem] * 7 + [in_any] * 6,
        out_specs=(in_vmem, in_vmem),
        scratch_shapes=scratch,
        compiler_params=pltpu.CompilerParams(
            collective_id=0, has_side_effects=True, vmem_limit_bytes=56 * 2**20
        ),
        name="vision_prefill_layer",
    )(
        tile_counts.reshape(1, n),
        text_lengths.reshape(1, n),
        page_table.reshape(1, n),
        patches,
        vision_gain,
        text_embed,
        attn_gain.reshape(n, 1, width),
        patch_weight,
        merger_inner.T,
        merger_weight,
        q_weight,
        kv_weight.T,
        out_weight,
    )
    return hidden, pool


def solution(mesh):
    in_specs = (
        P("groups"),
        P("groups"),
        P("groups"),
        P(("groups", "wide"), None, None),
        P(),
        P(),
        P(None, "wide"),
        P(None, "wide"),
        P("groups", "wide"),
        P(),
        P(None, "wide"),
        P(None, "wide"),
        P("wide", None),
    )
    out_specs = (P(("groups", "wide"), None), P(("groups", "wide"), None, None, None, None))
    return jax.shard_map(
        on_device, mesh=mesh, in_specs=in_specs, out_specs=out_specs, check_vma=False
    )
```

```python
import functools
import math

import jax
import jax.numpy as jnp
from jax import lax
from jax.experimental import pallas as pl
from jax.experimental.pallas import tpu as pltpu
from jax.sharding import PartitionSpec as P

HD = 128
TOK_DEV = 8
MAXT = 4
PAGE = 8
CHUNKS = 8
MESH = pl.DeviceIdType.MESH
F32 = jnp.float32
BF16 = jnp.bfloat16


def mm(a, b):
    return jnp.dot(a, b, preferred_element_type=F32)


def mm_t(a, b):
    return lax.dot_general(a, b, (((1,), (1,)), ((), ())), preferred_element_type=F32)


def iota(shape, dim):
    return lax.broadcasted_iota(jnp.int32, shape, dim)


def one_hot(condition):
    return jnp.where(condition, 1.0, 0.0).astype(BF16)


def slot_of(row, low_rows):
    high = row >= low_rows
    inner = jnp.where(high, row - low_rows, row)
    return (inner // MAXT) * TOK_DEV + inner % MAXT + jnp.where(high, MAXT, 0)


class Gather:
    def __init__(self, n, land, send, recv):
        me = lax.axis_index("wide")
        self.n, self.land, self.send, self.recv = n, land, send, recv
        self.depth = n // 4
        self.core, self.y, self.z = me % 2, (me // 2) % 2, me // 4
        self.me = me
        self.y_partner = self.index(self.z, 1 - self.y, self.core)
        self.sibling = self.index(self.z, self.y, 1 - self.core)

    def hop(self, step):
        common, bit = 0, 1
        while bit < self.depth:
            common = common + bit * ((self.z // bit) % 2) * ((step // bit) % 2)
            bit *= 2
        return self.z + step - 2 * common

    def index(self, z, y, core):
        return z * 4 + y * 2 + core

    def copy(self, block, slot, target):
        return pltpu.make_async_remote_copy(
            src_ref=self.land.at[block],
            dst_ref=self.land.at[block],
            send_sem=self.send.at[slot],
            recv_sem=self.recv.at[block],
            device_id={"wide": target},
            device_id_type=MESH,
        )

    def arrived(self, block):
        self.copy(block, 0, self.sibling).wait_recv()

    def start(self):
        depth = self.depth

        def along(step, carry):
            peer = self.index(self.hop(step), self.y, self.core)
            self.copy(self.me, step - 1, peer).start()
            return carry

        lax.fori_loop(1, depth, along, 0)
        self.copy(self.me, depth - 1, self.y_partner).start()
        self.copy(self.me, depth, self.sibling).start()

    def z_phase(self, use=None):
        depth = self.depth
        if use is not None:
            use(self.me)

        def step_of(step, carry):
            block = self.index(self.hop(step), self.y, self.core)
            self.arrived(block)
            self.copy(block, depth + step, self.y_partner).start()
            self.copy(block, 2 * depth - 1 + step, self.sibling).start()
            if use is not None:
                use(block)
            return carry

        lax.fori_loop(1, depth, step_of, 0)

    def y_phase(self, use=None):
        depth = self.depth

        def step_of(step, carry):
            block = self.index(self.hop(step), 1 - self.y, self.core)
            self.arrived(block)
            self.copy(block, 3 * depth - 1 + step, self.sibling).start()
            if use is not None:
                use(block)
            return carry

        lax.fori_loop(0, depth, step_of, 0)

    def core_phase(self, use=None):
        depth = self.depth
        for side in (self.y, 1 - self.y):

            def step_of(step, carry, side=side):
                block = self.index(self.hop(step), side, 1 - self.core)
                self.arrived(block)
                if use is not None:
                    use(block)
                return carry

            lax.fori_loop(0, depth, step_of, 0)

    def finish(self):
        def one(slot, carry):
            self.copy(self.me, slot, self.sibling).wait_send()
            return carry

        lax.fori_loop(0, self.n - 1, one, 0)


class GroupGather(Gather):
    def peer(self, step):
        return (self.me // 8) * 8 + (self.me + step) % 8

    def partner(self, step):
        groups = self.n // 8
        return ((self.me // 8 + step) % groups) * 8 + self.me % 8

    def spread(self, block, first):
        def one(step, carry):
            self.copy(block, first + step - 1, self.peer(step)).start()
            return carry

        lax.fori_loop(1, 8, one, 0)

    def start(self):
        self.spread(self.me, 0)
        for step in range(1, self.n // 8):
            self.copy(self.me, 6 + step, self.partner(step)).start()

    def wait_group(self):
        def one(step, carry):
            self.arrived(self.peer(step))
            return carry

        lax.fori_loop(1, 8, one, 0)

    def forward(self):
        groups = self.n // 8
        for step in range(1, groups):
            block = self.partner(step)
            self.arrived(block)
            self.spread(block, 6 + groups + (step - 1) * 7)

    def wait_others(self):
        groups = self.n // 8
        for step in range(1, groups):

            def one(i, carry, step=step):
                group = (self.me // 8 + step) % groups
                self.arrived(group * 8 + (self.me + i) % 8)
                return carry

            lax.fori_loop(1, 8, one, 0)


def layer_kernel(
    n,
    tiles_ref,
    lengths_ref,
    pages_ref,
    patches_ref,
    vgain_ref,
    text_ref,
    again_ref,
    pw_hbm,
    mi_hbm,
    mw_hbm,
    wq_hbm,
    wkv_hbm,
    ow_hbm,
    hidden_ref,
    pool_ref,
    pw,
    mi,
    mw,
    wq,
    wkv,
    ow,
    pixels,
    v_land,
    a_land,
    lo_land,
    hi_land,
    kv_land,
    vacc,
    qacc,
    kvacc,
    sqacc,
    ctx,
    home,
    part,
    ybuf,
    zsend,
    zbuf,
    own,
    fsend,
    frecv,
    w_sem,
    v_s,
    v_r,
    a_s,
    a_r,
    lo_s,
    lo_r,
    hi_s,
    hi_r,
    kv_s,
    kv_r,
    pair_s,
    pair_r,
    y_s,
    y_r,
    z_s,
    z_r,
    f_s,
    f_r,
):
    depth = n // 4
    me = lax.axis_index("wide")
    core, yy, zz = me % 2, (me // 2) % 2, me // 4
    low = n * MAXT
    slots = n * TOK_DEV
    width = text_ref.shape[1]
    inner = mi.shape[0]
    total_width = width * n
    half = total_width // 2
    cw = half // CHUNKS
    vis = vgain_ref.shape[0]

    gv = Gather(n, v_land, v_s, v_r)
    ga = Gather(n, a_land, a_s, a_r)
    glo = Gather(n, lo_land, lo_s, lo_r)
    ghi = Gather(n, hi_land, hi_s, hi_r)
    gkv = GroupGather(n, kv_land, kv_s, kv_r)
    y_partner, sibling = gv.y_partner, gv.sibling

    loads = [
        pltpu.make_async_copy(pw_hbm, pw, w_sem.at[0]),
        pltpu.make_async_copy(mi_hbm, mi, w_sem.at[1]),
        pltpu.make_async_copy(mw_hbm, mw, w_sem.at[2]),
        pltpu.make_async_copy(wq_hbm, wq, w_sem.at[3]),
        pltpu.make_async_copy(wkv_hbm, wkv, w_sem.at[4]),
        pltpu.make_async_copy(
            ow_hbm.at[:, pl.ds(pl.multiple_of(core * half, half), half)], ow.at[core], w_sem.at[5]
        ),
    ]
    loads[0].start()

    barrier = pltpu.get_barrier_semaphore()

    def greet(step, carry):
        peer = (me + step) % n
        pl.semaphore_signal(barrier, inc=1, device_id={"wide": peer}, device_id_type=MESH)
        return carry

    lax.fori_loop(1, n, greet, 0)

    for tile in range(patches_ref.shape[0]):
        pixels[tile * 4 : tile * 4 + 4] = patches_ref[tile].astype(F32)
    loads[0].wait()
    for load in loads[1:]:
        load.start()
    embedded = mm(pixels[...].astype(BF16), pw[...])
    centred = embedded - jnp.mean(embedded, axis=1, keepdims=True)
    variance = jnp.mean(centred * centred, axis=1, keepdims=True)
    v_land[me] = (centred * lax.rsqrt(variance + 1e-06) * vgain_ref[...].reshape(1, vis)).astype(BF16)
    order = one_hot(slot_of(iota((slots, slots), 0), low) == iota((slots, slots), 1))
    text_rows = mm(order, text_ref[...])
    hi_land[me] = text_rows[low:].astype(BF16)

    pl.semaphore_wait(barrier, n - 1)
    gv.start()
    ghi.start()
    ow_copy = pltpu.make_async_remote_copy(
        src_ref=ow_hbm.at[:, pl.ds(pl.multiple_of((1 - core) * half, half), half)],
        dst_ref=ow.at[core],
        send_sem=pair_s.at[0],
        recv_sem=pair_r.at[0],
        device_id={"wide": sibling},
        device_id_type=MESH,
    )
    gv.z_phase()
    gv.y_phase()
    gv.core_phase()
    ghi.z_phase()

    loads[1].wait()
    every = v_land[...].reshape(n * 16, vis)
    tile_row, patch_row = iota((low, n * 16), 0), iota((low, n * 16), 1)
    lifted = jnp.zeros((low, inner), F32)
    for p in range(4):
        pick = one_hot(patch_row == tile_row * 4 + p)
        lifted = lifted + mm_t(mm(pick, every).astype(BF16), mi[:, p * vis : (p + 1) * vis])
    a_land[me] = (0.5 * lifted * (1.0 + lax.erf(lifted * math.sqrt(0.5)))).astype(BF16)
    ga.start()

    loads[2].wait()
    vacc[...] = jnp.zeros_like(vacc)

    def merge(block):
        rows = pl.ds(pl.multiple_of(block * inner, 16), inner)
        vacc[...] += mm(a_land[block], mw[rows, :])

    ga.z_phase(merge)
    ga.y_phase(merge)
    ga.core_phase(merge)

    owner_low = iota((low, n), 0) // MAXT == iota((low, n), 1)
    tiles_low = jnp.sum(
        jnp.where(owner_low, tiles_ref[...].astype(F32), 0.0), axis=1, keepdims=True
    )
    is_vision = (iota((low, 1), 0) % MAXT).astype(F32) < tiles_low
    vision = vacc[...].astype(BF16).astype(F32)
    lo_land[me] = jnp.where(is_vision, vision, text_rows[:low]).astype(BF16)
    glo.start()
    ow_copy.start()

    loads[3].wait()
    loads[4].wait()
    qacc[...] = jnp.zeros_like(qacc)
    kvacc[...] = jnp.zeros_like(kvacc)
    sqacc[...] = jnp.zeros_like(sqacc)

    def project(which, land):
        def use(block):
            x = land[block].astype(F32)
            sqacc[which] += jnp.sum(x * x, axis=1, keepdims=True)
            scaled = (x * again_ref[block]).astype(BF16)
            span = pl.ds(pl.multiple_of(block * width, 128), width)
            qacc[which] += mm(scaled, wq[span, :])
            kvacc[which] += mm_t(wkv[:, span], scaled)

        return use

    ghi.y_phase(project(1, hi_land))
    glo.z_phase(project(0, lo_land))
    glo.y_phase(project(0, lo_land))
    ghi_use = project(1, hi_land)
    ghi_use(me)

    def behind(step, carry):
        ghi_use(ghi.index(ghi.hop(step), yy, core))
        return carry

    lax.fori_loop(1, depth, behind, 0)
    ghi.core_phase(ghi_use)
    glo.core_phase(project(0, lo_land))

    queries = jnp.zeros((slots, HD), F32)
    keyvals = jnp.zeros((kvacc.shape[1], slots), F32)
    eye = iota((low, low), 0) == iota((low, low), 1)
    for which in range(2):
        scale = lax.rsqrt(sqacc[which] * (1.0 / total_width) + 1e-06)
        across = jnp.sum(jnp.where(eye, scale, 0.0), axis=0, keepdims=True)
        slot_col = slot_of(iota((low, slots), 0) + which * low, low)
        to_slot = one_hot(slot_col == iota((low, slots), 1))
        keyvals = keyvals + mm((kvacc[which] * across).astype(BF16), to_slot)
        slot_row = slot_of(iota((slots, low), 1) + which * low, low)
        from_slot = one_hot(slot_row == iota((slots, low), 0))
        queries = queries + mm(from_slot, (qacc[which] * scale).astype(BF16))
    kv_land[me] = keyvals.astype(BF16)
    gkv.start()
    queries = queries.astype(BF16)

    chip = me // 2
    wanted = chip * 16 + iota((16, low), 0)
    pick_lo = one_hot(slot_of(iota((16, low), 1), low) == wanted)
    pick_hi = one_hot(slot_of(iota((16, low), 1) + low, low) == wanted)

    def residual(step, carry):
        block = core * (n // 2) + step
        rows = mm(pick_lo, lo_land[block]) + mm(pick_hi, hi_land[block])
        home[:, pl.ds(pl.multiple_of(step * width, 128), width)] = rows
        return carry

    lax.fori_loop(0, n // 2, residual, 0)
    gkv.wait_group()

    group = me // 8
    keys_t = kv_land[pl.ds(group * 8, 4)].reshape(HD, slots)
    values_t = kv_land[pl.ds(group * 8 + 4, 4)].reshape(HD, slots)
    q_pos, k_pos = iota((slots, slots), 0), iota((slots, slots), 1)
    owner = iota((slots, n), 0) // TOK_DEV == iota((slots, n), 1)
    count_row = (tiles_ref[...] + lengths_ref[...]).astype(F32)
    count = jnp.sum(jnp.where(owner, count_row, 0.0), axis=1, keepdims=True)
    live = (iota((slots, 1), 0) % TOK_DEV).astype(F32) < count
    same = (q_pos // TOK_DEV == k_pos // TOK_DEV) & (k_pos <= q_pos)
    floor = jnp.float32(-1e30)
    scores = mm(queries, keys_t) * (1.0 / math.sqrt(HD))
    within = jnp.where(live, jnp.where(same, scores, floor), floor)
    scores = jnp.where(q_pos == k_pos, scores, within)
    weights = jnp.exp(scores - jnp.max(scores, axis=1, keepdims=True))
    probs = (weights / jnp.sum(weights, axis=1, keepdims=True)).astype(BF16)
    ctx[core] = mm_t(probs, values_t).astype(BF16)
    ctx_copy = pltpu.make_async_remote_copy(
        src_ref=ctx.at[core],
        dst_ref=ctx.at[core],
        send_sem=pair_s.at[1],
        recv_sem=pair_r.at[1],
        device_id={"wide": sibling},
        device_id_type=MESH,
    )
    ctx_copy.start()

    gkv.forward()

    loads[5].wait()
    ow_copy.wait_recv()
    ctx_copy.wait_recv()

    both = jnp.concatenate([ctx[0], ctx[1]], axis=1)

    def y_copy(k):
        return pltpu.make_async_remote_copy(
            src_ref=part.at[k, 1 - yy],
            dst_ref=ybuf.at[k],
            send_sem=y_s.at[k],
            recv_sem=y_r.at[k],
            device_id={"wide": y_partner},
            device_id_type=MESH,
        )

    def z_copy(k, step):
        peer_z = (zz + step) % depth
        return pltpu.make_async_remote_copy(
            src_ref=zsend.at[k, peer_z],
            dst_ref=zbuf.at[k, step],
            send_sem=z_s.at[k, step],
            recv_sem=z_r.at[k, step],
            device_id={"wide": peer_z * 4 + yy * 2 + core},
            device_id_type=MESH,
        )

    def f_copy(k):
        return pltpu.make_async_remote_copy(
            src_ref=fsend.at[k],
            dst_ref=frecv.at[k],
            send_sem=f_s.at[k],
            recv_sem=f_r.at[k],
            device_id={"wide": sibling},
            device_id_type=MESH,
        )

    for k in range(CHUNKS):
        cols = slice(k * cw, (k + 1) * cw)
        share = mm(both, ow[:, :, cols].reshape(2 * HD, cw)).astype(BF16)
        for z in range(depth):
            for y in range(2):
                row = (z * 2 + y) * 16
                part[k, y, z] = share[row : row + 16]
        y_copy(k).start()

    for k in range(CHUNKS):
        y_copy(k).wait_recv()
        for step in range(1, depth):
            peer_z = (zz + step) % depth
            summed = part[k, yy, peer_z].astype(F32) + ybuf[k, peer_z].astype(F32)
            zsend[k, peer_z] = summed.astype(BF16)
            z_copy(k, step).start()
        own[k] = (
            part[k, yy, zz].astype(F32)
            + ybuf[k, zz].astype(F32)
            + home[:, k * cw : (k + 1) * cw]
        )
    gkv.wait_others()
    mine = jnp.where(pages_ref[...] == me, 1.0, 0.0)
    mine_rows = jnp.broadcast_to(mine, (PAGE, n)).astype(BF16)
    spread = one_hot(iota((n, slots), 0) == iota((n, slots), 1) // PAGE)
    in_page = iota((PAGE, slots), 1) % PAGE == iota((PAGE, slots), 0)
    chosen = jnp.where(in_page, mm(mine_rows, spread), 0.0).astype(BF16)
    for g in range(n // 8):
        for kind in range(2):
            first = g * 8 + kind * 4
            rows_t = kv_land[first : first + 4].reshape(HD, slots)
            pool_ref[0, kind, g] = mm_t(chosen, rows_t).astype(BF16)

    is_first = core == 0
    for k in range(CHUNKS):
        rows = own[k]
        for step in range(1, depth):
            z_copy(k, step).wait_recv()
            rows = rows + zbuf[k, step].astype(F32)
        upper, lower = rows[:TOK_DEV], rows[TOK_DEV:]
        fsend[k] = jnp.where(is_first, lower, upper).astype(BF16)
        f_copy(k).start()
        kept = jnp.where(is_first, upper, lower).astype(BF16)
        hidden_ref[:, pl.ds(pl.multiple_of(core * half + k * cw, 128), cw)] = kept
    for k in range(CHUNKS):
        f_copy(k).wait_recv()
        hidden_ref[:, pl.ds(pl.multiple_of((1 - core) * half + k * cw, 128), cw)] = frecv[k]

    ow_copy.wait_send()
    ctx_copy.wait_send()
    for k in range(CHUNKS):
        y_copy(k).wait_send()
        f_copy(k).wait_send()
        for step in range(1, depth):
            z_copy(k, step).wait_send()
    for gather in (gv, ga, glo, ghi, gkv):
        gather.finish()


def on_device(
    tile_counts,
    text_lengths,
    page_table,
    patches,
    patch_weight,
    vision_gain,
    merger_inner,
    merger_weight,
    text_embed,
    attn_gain,
    q_weight,
    kv_weight,
    out_weight,
):
    n = lax.axis_size("wide")
    depth = n // 4
    slots = n * TOK_DEV
    low = n * MAXT
    width = text_embed.shape[1]
    inner = merger_inner.shape[1]
    total_width = width * n
    half = total_width // 2
    cw = half // CHUNKS
    kv_cols = kv_weight.shape[1]
    vis = patch_weight.shape[1]
    dma = pltpu.SemaphoreType.DMA
    in_vmem = pl.BlockSpec(memory_space=pltpu.VMEM)
    in_any = pl.BlockSpec(memory_space=pl.ANY)
    scratch = [
        pltpu.VMEM(patch_weight.shape, BF16),
        pltpu.VMEM((inner, merger_inner.shape[0]), BF16),
        pltpu.VMEM(merger_weight.shape, BF16),
        pltpu.VMEM(q_weight.shape, BF16),
        pltpu.VMEM((kv_cols, total_width), BF16),
        pltpu.VMEM((2, HD, half), BF16),
        pltpu.VMEM((16, patch_weight.shape[0]), F32),
        pltpu.VMEM((n, 16, vis), BF16),
        pltpu.VMEM((n, low, inner), BF16),
        pltpu.VMEM((n, low, width), BF16),
        pltpu.VMEM((n, low, width), BF16),
        pltpu.VMEM((n, kv_cols, slots), BF16),
        pltpu.VMEM((low, width), F32),
        pltpu.VMEM((2, low, HD), F32),
        pltpu.VMEM((2, kv_cols, low), F32),
        pltpu.VMEM((2, low, 1), F32),
        pltpu.VMEM((2, slots, HD), BF16),
        pltpu.VMEM((16, half), F32),
        pltpu.VMEM((CHUNKS, 2, depth, 16, cw), BF16),
        pltpu.VMEM((CHUNKS, depth, 16, cw), BF16),
        pltpu.VMEM((CHUNKS, depth, 16, cw), BF16),
        pltpu.VMEM((CHUNKS, depth, 16, cw), BF16),
        pltpu.VMEM((CHUNKS, 16, cw), F32),
        pltpu.VMEM((CHUNKS, TOK_DEV, cw), BF16),
        pltpu.VMEM((CHUNKS, TOK_DEV, cw), BF16),
        dma((6,)),
    ]
    for _ in range(5):
        scratch += [dma((n,)), dma((n,))]
    scratch += [dma((2,)), dma((2,)), dma((CHUNKS,)), dma((CHUNKS,))]
    scratch += [dma((CHUNKS, depth)), dma((CHUNKS, depth)), dma((CHUNKS,)), dma((CHUNKS,))]
    hidden, pool = pl.pallas_call(
        functools.partial(layer_kernel, n),
        out_shape=(
            jax.ShapeDtypeStruct((TOK_DEV, total_width), BF16),
            jax.ShapeDtypeStruct((1, 2, n // 8, PAGE, HD), BF16),
        ),
        in_specs=[in_vmem] * 7 + [in_any] * 6,
        out_specs=(in_vmem, in_vmem),
        scratch_shapes=scratch,
        compiler_params=pltpu.CompilerParams(
            collective_id=0, has_side_effects=True, vmem_limit_bytes=56 * 2**20
        ),
        name="vision_prefill_layer",
    )(
        tile_counts.reshape(1, n),
        text_lengths.reshape(1, n),
        page_table.reshape(1, n),
        patches,
        vision_gain,
        text_embed,
        attn_gain.reshape(n, 1, width),
        patch_weight,
        merger_inner.T,
        merger_weight,
        q_weight,
        kv_weight.T,
        out_weight,
    )
    return hidden, pool


def solution(mesh):
    in_specs = (
        P("groups"),
        P("groups"),
        P("groups"),
        P(("groups", "wide"), None, None),
        P(),
        P(),
        P(None, "wide"),
        P(None, "wide"),
        P("groups", "wide"),
        P(),
        P(None, "wide"),
        P(None, "wide"),
        P("wide", None),
    )
    out_specs = (P(("groups", "wide"), None), P(("groups", "wide"), None, None, None, None))
    return jax.shard_map(
        on_device, mesh=mesh, in_specs=in_specs, out_specs=out_specs, check_vma=False
    )
```

```python
import functools
import math

import jax
import jax.numpy as jnp
from jax import lax
from jax.experimental import pallas as pl
from jax.experimental.pallas import tpu as pltpu
from jax.sharding import PartitionSpec as P

HD = 128
TOK_DEV = 8
MAXT = 4
PAGE = 8
CHUNKS = 8
MESH = pl.DeviceIdType.MESH
F32 = jnp.float32
BF16 = jnp.bfloat16


def mm(a, b):
    return jnp.dot(a, b, preferred_element_type=F32)


def mm_t(a, b):
    return lax.dot_general(a, b, (((1,), (1,)), ((), ())), preferred_element_type=F32)


def iota(shape, dim):
    return lax.broadcasted_iota(jnp.int32, shape, dim)


def one_hot(condition):
    return jnp.where(condition, 1.0, 0.0).astype(BF16)


def slot_of(row, low_rows):
    high = row >= low_rows
    inner = jnp.where(high, row - low_rows, row)
    return (inner // MAXT) * TOK_DEV + inner % MAXT + jnp.where(high, MAXT, 0)


class Gather:
    def __init__(self, n, land, send, recv):
        me = lax.axis_index("wide")
        self.n, self.land, self.send, self.recv = n, land, send, recv
        self.depth = n // 4
        self.core, self.y, self.z = me % 2, (me // 2) % 2, me // 4
        self.me = me
        self.y_partner = self.index(self.z, 1 - self.y, self.core)
        self.sibling = self.index(self.z, self.y, 1 - self.core)

    def hop(self, step):
        common, bit = 0, 1
        while bit < self.depth:
            common = common + bit * ((self.z // bit) % 2) * ((step // bit) % 2)
            bit *= 2
        return self.z + step - 2 * common

    def index(self, z, y, core):
        return z * 4 + y * 2 + core

    def copy(self, block, slot, target):
        return pltpu.make_async_remote_copy(
            src_ref=self.land.at[block],
            dst_ref=self.land.at[block],
            send_sem=self.send.at[slot],
            recv_sem=self.recv.at[block],
            device_id={"wide": target},
            device_id_type=MESH,
        )

    def arrived(self, block):
        self.copy(block, 0, self.sibling).wait_recv()

    def start(self):
        depth = self.depth

        def along(step, carry):
            peer = self.index(self.hop(step), self.y, self.core)
            self.copy(self.me, step - 1, peer).start()
            return carry

        lax.fori_loop(1, depth, along, 0)
        self.copy(self.me, depth - 1, self.y_partner).start()
        self.copy(self.me, depth, self.sibling).start()

    def z_phase(self, use=None):
        depth = self.depth
        if use is not None:
            use(self.me)

        def step_of(step, carry):
            block = self.index(self.hop(step), self.y, self.core)
            self.arrived(block)
            self.copy(block, depth + step, self.y_partner).start()
            self.copy(block, 2 * depth - 1 + step, self.sibling).start()
            if use is not None:
                use(block)
            return carry

        lax.fori_loop(1, depth, step_of, 0)

    def y_phase(self, use=None):
        depth = self.depth

        def step_of(step, carry):
            block = self.index(self.hop(step), 1 - self.y, self.core)
            self.arrived(block)
            self.copy(block, 3 * depth - 1 + step, self.sibling).start()
            if use is not None:
                use(block)
            return carry

        lax.fori_loop(0, depth, step_of, 0)

    def core_phase(self, use=None):
        depth = self.depth
        for side in (self.y, 1 - self.y):

            def step_of(step, carry, side=side):
                block = self.index(self.hop(step), side, 1 - self.core)
                self.arrived(block)
                if use is not None:
                    use(block)
                return carry

            lax.fori_loop(0, depth, step_of, 0)

    def finish(self):
        def one(slot, carry):
            self.copy(self.me, slot, self.sibling).wait_send()
            return carry

        lax.fori_loop(0, self.n - 1, one, 0)


class GroupGather(Gather):
    def peer(self, step):
        return (self.me // 8) * 8 + (self.me + step) % 8

    def partner(self, step):
        groups = self.n // 8
        return ((self.me // 8 + step) % groups) * 8 + self.me % 8

    def spread(self, block, first):
        def one(step, carry):
            self.copy(block, first + step - 1, self.peer(step)).start()
            return carry

        lax.fori_loop(1, 8, one, 0)

    def start(self):
        self.spread(self.me, 0)
        for step in range(1, self.n // 8):
            self.copy(self.me, 6 + step, self.partner(step)).start()

    def wait_group(self):
        def one(step, carry):
            self.arrived(self.peer(step))
            return carry

        lax.fori_loop(1, 8, one, 0)

    def forward(self):
        groups = self.n // 8
        for step in range(1, groups):
            block = self.partner(step)
            self.arrived(block)
            self.spread(block, 6 + groups + (step - 1) * 7)

    def wait_others(self):
        groups = self.n // 8
        for step in range(1, groups):

            def one(i, carry, step=step):
                group = (self.me // 8 + step) % groups
                self.arrived(group * 8 + (self.me + i) % 8)
                return carry

            lax.fori_loop(1, 8, one, 0)


def layer_kernel(
    n,
    tiles_ref,
    lengths_ref,
    pages_ref,
    patches_ref,
    vgain_ref,
    text_ref,
    again_ref,
    pw_hbm,
    mi_hbm,
    mw_hbm,
    wq_hbm,
    wkv_hbm,
    ow_hbm,
    hidden_ref,
    pool_ref,
    pw,
    mi,
    mw,
    wq,
    wkv,
    ow,
    pixels,
    v_land,
    a_land,
    lo_land,
    hi_land,
    kv_land,
    vacc,
    qacc,
    kvacc,
    sqacc,
    ctx,
    home,
    part,
    ybuf,
    zsend,
    zbuf,
    own,
    fsend,
    frecv,
    w_sem,
    v_s,
    v_r,
    a_s,
    a_r,
    lo_s,
    lo_r,
    hi_s,
    hi_r,
    kv_s,
    kv_r,
    pair_s,
    pair_r,
    y_s,
    y_r,
    z_s,
    z_r,
    f_s,
    f_r,
):
    depth = n // 4
    me = lax.axis_index("wide")
    core, yy, zz = me % 2, (me // 2) % 2, me // 4
    low = n * MAXT
    slots = n * TOK_DEV
    width = text_ref.shape[1]
    inner = mi.shape[0]
    total_width = width * n
    half = total_width // 2
    cw = half // CHUNKS
    vis = vgain_ref.shape[0]

    gv = Gather(n, v_land, v_s, v_r)
    ga = Gather(n, a_land, a_s, a_r)
    glo = Gather(n, lo_land, lo_s, lo_r)
    ghi = Gather(n, hi_land, hi_s, hi_r)
    gkv = GroupGather(n, kv_land, kv_s, kv_r)
    y_partner, sibling = gv.y_partner, gv.sibling

    loads = [
        pltpu.make_async_copy(pw_hbm, pw, w_sem.at[0]),
        pltpu.make_async_copy(mi_hbm, mi, w_sem.at[1]),
        pltpu.make_async_copy(mw_hbm, mw, w_sem.at[2]),
        pltpu.make_async_copy(wq_hbm, wq, w_sem.at[3]),
        pltpu.make_async_copy(wkv_hbm, wkv, w_sem.at[4]),
        pltpu.make_async_copy(
            ow_hbm.at[:, pl.ds(pl.multiple_of(core * half, half), half)], ow.at[core], w_sem.at[5]
        ),
    ]
    loads[0].start()

    barrier = pltpu.get_barrier_semaphore()

    def greet(step, carry):
        peer = (me + step) % n
        pl.semaphore_signal(barrier, inc=1, device_id={"wide": peer}, device_id_type=MESH)
        return carry

    lax.fori_loop(1, n, greet, 0)

    for tile in range(patches_ref.shape[0]):
        pixels[tile * 4 : tile * 4 + 4] = patches_ref[tile].astype(F32)
    loads[0].wait()
    for load in loads[1:]:
        load.start()
    embedded = mm(pixels[...].astype(BF16), pw[...])
    centred = embedded - jnp.mean(embedded, axis=1, keepdims=True)
    variance = jnp.mean(centred * centred, axis=1, keepdims=True)
    v_land[me] = (centred * lax.rsqrt(variance + 1e-06) * vgain_ref[...].reshape(1, vis)).astype(BF16)
    order = one_hot(slot_of(iota((slots, slots), 0), low) == iota((slots, slots), 1))
    text_rows = mm(order, text_ref[...])
    hi_land[me] = text_rows[low:].astype(BF16)

    pl.semaphore_wait(barrier, n - 1)
    gv.start()
    ghi.start()
    ow_copy = pltpu.make_async_remote_copy(
        src_ref=ow_hbm.at[:, pl.ds(pl.multiple_of((1 - core) * half, half), half)],
        dst_ref=ow.at[core],
        send_sem=pair_s.at[0],
        recv_sem=pair_r.at[0],
        device_id={"wide": sibling},
        device_id_type=MESH,
    )
    sorted_row = iota((n * 16, n * 16), 0)
    pick = one_hot(iota((n * 16, n * 16), 1) == sorted_row % low * 4 + sorted_row // low)
    gv.z_phase()
    gv.y_phase()
    gv.core_phase()
    ghi.z_phase()

    loads[1].wait()
    every = v_land[...].reshape(n * 16, vis)
    by_patch = mm(pick, every).astype(BF16)
    lifted = jnp.zeros((low, inner), F32)
    for p in range(4):
        lifted = lifted + mm_t(by_patch[p * low : (p + 1) * low], mi[:, p * vis : (p + 1) * vis])
    a_land[me] = (0.5 * lifted * (1.0 + lax.erf(lifted * math.sqrt(0.5)))).astype(BF16)
    ga.start()

    loads[2].wait()
    vacc[...] = jnp.zeros_like(vacc)

    def merge(block):
        rows = pl.ds(pl.multiple_of(block * inner, 16), inner)
        vacc[...] += mm(a_land[block], mw[rows, :])

    owner_low = iota((low, n), 0) // MAXT == iota((low, n), 1)
    tiles_low = jnp.sum(
        jnp.where(owner_low, tiles_ref[...].astype(F32), 0.0), axis=1, keepdims=True
    )
    is_vision = (iota((low, 1), 0) % MAXT).astype(F32) < tiles_low
    ga.z_phase(merge)
    ga.y_phase(merge)
    ga.core_phase(merge)

    vision = vacc[...].astype(BF16).astype(F32)
    lo_land[me] = jnp.where(is_vision, vision, text_rows[:low]).astype(BF16)
    glo.start()
    ow_copy.start()

    loads[3].wait()
    loads[4].wait()
    qacc[...] = jnp.zeros_like(qacc)
    kvacc[...] = jnp.zeros_like(kvacc)
    sqacc[...] = jnp.zeros_like(sqacc)

    def project(which, land):
        def use(block):
            x = land[block].astype(F32)
            sqacc[which] += jnp.sum(x * x, axis=1, keepdims=True)
            scaled = (x * again_ref[block]).astype(BF16)
            span = pl.ds(pl.multiple_of(block * width, 128), width)
            qacc[which] += mm(scaled, wq[span, :])
            kvacc[which] += mm_t(wkv[:, span], scaled)

        return use

    ghi.y_phase(project(1, hi_land))
    glo.z_phase(project(0, lo_land))
    ghi_use, glo_use = project(1, hi_land), project(0, lo_land)

    def both_halves(block):
        glo_use(block)
        ghi_use(block + 2 - 4 * ((block // 2) % 2))

    glo.y_phase(both_halves)
    ghi.core_phase(ghi_use)
    sums = [jnp.zeros((kvacc.shape[1], slots), F32), jnp.zeros((slots, HD), F32)]
    eye = iota((low, low), 0) == iota((low, low), 1)

    def add_rows(which):
        scale = lax.rsqrt(sqacc[which] * (1.0 / total_width) + 1e-06)
        across = jnp.sum(jnp.where(eye, scale, 0.0), axis=0, keepdims=True)
        slot_col = slot_of(iota((low, slots), 0) + which * low, low)
        to_slot = one_hot(slot_col == iota((low, slots), 1))
        sums[0] = sums[0] + mm((kvacc[which] * across).astype(BF16), to_slot)
        slot_row = slot_of(iota((slots, low), 1) + which * low, low)
        from_slot = one_hot(slot_row == iota((slots, low), 0))
        sums[1] = sums[1] + mm(from_slot, (qacc[which] * scale).astype(BF16))

    add_rows(1)
    glo.core_phase(project(0, lo_land))

    add_rows(0)
    keyvals, queries = sums
    kv_land[me] = keyvals.astype(BF16)
    gkv.start()
    queries = queries.astype(BF16)

    chip = me // 2
    wanted = chip * 16 + iota((16, low), 0)
    pick_lo = one_hot(slot_of(iota((16, low), 1), low) == wanted)
    pick_hi = one_hot(slot_of(iota((16, low), 1) + low, low) == wanted)

    def residual(step, carry):
        block = core * (n // 2) + step
        rows = mm(pick_lo, lo_land[block]) + mm(pick_hi, hi_land[block])
        home[:, pl.ds(pl.multiple_of(step * width, 128), width)] = rows
        return carry

    lax.fori_loop(0, n // 2, residual, 0)
    q_pos, k_pos = iota((slots, slots), 0), iota((slots, slots), 1)
    owner = iota((slots, n), 0) // TOK_DEV == iota((slots, n), 1)
    count_row = (tiles_ref[...] + lengths_ref[...]).astype(F32)
    count = jnp.sum(jnp.where(owner, count_row, 0.0), axis=1, keepdims=True)
    live = (iota((slots, 1), 0) % TOK_DEV).astype(F32) < count
    same = (q_pos // TOK_DEV == k_pos // TOK_DEV) & (k_pos <= q_pos)
    floor = jnp.float32(-1e30)
    gkv.wait_group()

    group = me // 8
    keys_t = kv_land[pl.ds(group * 8, 4)].reshape(HD, slots)
    values_t = kv_land[pl.ds(group * 8 + 4, 4)].reshape(HD, slots)
    scores = mm(queries, keys_t) * (1.0 / math.sqrt(HD))
    within = jnp.where(live, jnp.where(same, scores, floor), floor)
    scores = jnp.where(q_pos == k_pos, scores, within)
    weights = jnp.exp(scores - jnp.max(scores, axis=1, keepdims=True))
    probs = (weights / jnp.sum(weights, axis=1, keepdims=True)).astype(BF16)
    ctx[core] = mm_t(probs, values_t).astype(BF16)
    ctx_copy = pltpu.make_async_remote_copy(
        src_ref=ctx.at[core],
        dst_ref=ctx.at[core],
        send_sem=pair_s.at[1],
        recv_sem=pair_r.at[1],
        device_id={"wide": sibling},
        device_id_type=MESH,
    )
    ctx_copy.start()

    gkv.forward()

    loads[5].wait()
    ow_copy.wait_recv()
    ctx_copy.wait_recv()

    both = jnp.concatenate([ctx[0], ctx[1]], axis=1)

    def y_copy(k):
        return pltpu.make_async_remote_copy(
            src_ref=part.at[k, 1 - yy],
            dst_ref=ybuf.at[k],
            send_sem=y_s.at[k],
            recv_sem=y_r.at[k],
            device_id={"wide": y_partner},
            device_id_type=MESH,
        )

    def z_copy(k, step):
        peer_z = (zz + step) % depth
        return pltpu.make_async_remote_copy(
            src_ref=zsend.at[k, peer_z],
            dst_ref=zbuf.at[k, step],
            send_sem=z_s.at[k, step],
            recv_sem=z_r.at[k, step],
            device_id={"wide": peer_z * 4 + yy * 2 + core},
            device_id_type=MESH,
        )

    def f_copy(k):
        return pltpu.make_async_remote_copy(
            src_ref=fsend.at[k],
            dst_ref=frecv.at[k],
            send_sem=f_s.at[k],
            recv_sem=f_r.at[k],
            device_id={"wide": sibling},
            device_id_type=MESH,
        )

    for k in range(CHUNKS):
        cols = slice(k * cw, (k + 1) * cw)
        share = mm(both, ow[:, :, cols].reshape(2 * HD, cw)).astype(BF16)
        for z in range(depth):
            for y in range(2):
                row = (z * 2 + y) * 16
                part[k, y, z] = share[row : row + 16]
        y_copy(k).start()

    for k in range(CHUNKS):
        y_copy(k).wait_recv()
        for step in range(1, depth):
            peer_z = (zz + step) % depth
            summed = part[k, yy, peer_z].astype(F32) + ybuf[k, peer_z].astype(F32)
            zsend[k, peer_z] = summed.astype(BF16)
            z_copy(k, step).start()
        own[k] = (
            part[k, yy, zz].astype(F32)
            + ybuf[k, zz].astype(F32)
            + home[:, k * cw : (k + 1) * cw]
        )
    gkv.wait_others()
    mine = jnp.where(pages_ref[...] == me, 1.0, 0.0)
    mine_rows = jnp.broadcast_to(mine, (PAGE, n)).astype(BF16)
    spread = one_hot(iota((n, slots), 0) == iota((n, slots), 1) // PAGE)
    in_page = iota((PAGE, slots), 1) % PAGE == iota((PAGE, slots), 0)
    chosen = jnp.where(in_page, mm(mine_rows, spread), 0.0).astype(BF16)
    for g in range(n // 8):
        for kind in range(2):
            first = g * 8 + kind * 4
            rows_t = kv_land[first : first + 4].reshape(HD, slots)
            pool_ref[0, kind, g] = mm_t(chosen, rows_t).astype(BF16)

    is_first = core == 0
    for k in range(CHUNKS):
        rows = own[k]
        for step in range(1, depth):
            z_copy(k, step).wait_recv()
            rows = rows + zbuf[k, step].astype(F32)
        upper, lower = rows[:TOK_DEV], rows[TOK_DEV:]
        fsend[k] = jnp.where(is_first, lower, upper).astype(BF16)
        f_copy(k).start()
        kept = jnp.where(is_first, upper, lower).astype(BF16)
        hidden_ref[:, pl.ds(pl.multiple_of(core * half + k * cw, 128), cw)] = kept
    for k in range(CHUNKS):
        f_copy(k).wait_recv()
        hidden_ref[:, pl.ds(pl.multiple_of((1 - core) * half + k * cw, 128), cw)] = frecv[k]

    ow_copy.wait_send()
    ctx_copy.wait_send()
    for k in range(CHUNKS):
        y_copy(k).wait_send()
        f_copy(k).wait_send()
        for step in range(1, depth):
            z_copy(k, step).wait_send()
    for gather in (gv, ga, glo, ghi, gkv):
        gather.finish()


def on_device(
    tile_counts,
    text_lengths,
    page_table,
    patches,
    patch_weight,
    vision_gain,
    merger_inner,
    merger_weight,
    text_embed,
    attn_gain,
    q_weight,
    kv_weight,
    out_weight,
):
    n = lax.axis_size("wide")
    depth = n // 4
    slots = n * TOK_DEV
    low = n * MAXT
    width = text_embed.shape[1]
    inner = merger_inner.shape[1]
    total_width = width * n
    half = total_width // 2
    cw = half // CHUNKS
    kv_cols = kv_weight.shape[1]
    vis = patch_weight.shape[1]
    dma = pltpu.SemaphoreType.DMA
    in_vmem = pl.BlockSpec(memory_space=pltpu.VMEM)
    in_any = pl.BlockSpec(memory_space=pl.ANY)
    scratch = [
        pltpu.VMEM(patch_weight.shape, BF16),
        pltpu.VMEM((inner, merger_inner.shape[0]), BF16),
        pltpu.VMEM(merger_weight.shape, BF16),
        pltpu.VMEM(q_weight.shape, BF16),
        pltpu.VMEM((kv_cols, total_width), BF16),
        pltpu.VMEM((2, HD, half), BF16),
        pltpu.VMEM((16, patch_weight.shape[0]), F32),
        pltpu.VMEM((n, 16, vis), BF16),
        pltpu.VMEM((n, low, inner), BF16),
        pltpu.VMEM((n, low, width), BF16),
        pltpu.VMEM((n, low, width), BF16),
        pltpu.VMEM((n, kv_cols, slots), BF16),
        pltpu.VMEM((low, width), F32),
        pltpu.VMEM((2, low, HD), F32),
        pltpu.VMEM((2, kv_cols, low), F32),
        pltpu.VMEM((2, low, 1), F32),
        pltpu.VMEM((2, slots, HD), BF16),
        pltpu.VMEM((16, half), F32),
        pltpu.VMEM((CHUNKS, 2, depth, 16, cw), BF16),
        pltpu.VMEM((CHUNKS, depth, 16, cw), BF16),
        pltpu.VMEM((CHUNKS, depth, 16, cw), BF16),
        pltpu.VMEM((CHUNKS, depth, 16, cw), BF16),
        pltpu.VMEM((CHUNKS, 16, cw), F32),
        pltpu.VMEM((CHUNKS, TOK_DEV, cw), BF16),
        pltpu.VMEM((CHUNKS, TOK_DEV, cw), BF16),
        dma((6,)),
    ]
    for _ in range(5):
        scratch += [dma((n,)), dma((n,))]
    scratch += [dma((2,)), dma((2,)), dma((CHUNKS,)), dma((CHUNKS,))]
    scratch += [dma((CHUNKS, depth)), dma((CHUNKS, depth)), dma((CHUNKS,)), dma((CHUNKS,))]
    hidden, pool = pl.pallas_call(
        functools.partial(layer_kernel, n),
        out_shape=(
            jax.ShapeDtypeStruct((TOK_DEV, total_width), BF16),
            jax.ShapeDtypeStruct((1, 2, n // 8, PAGE, HD), BF16),
        ),
        in_specs=[in_vmem] * 7 + [in_any] * 6,
        out_specs=(in_vmem, in_vmem),
        scratch_shapes=scratch,
        compiler_params=pltpu.CompilerParams(
            collective_id=0, has_side_effects=True, vmem_limit_bytes=56 * 2**20
        ),
        name="vision_prefill_layer",
    )(
        tile_counts.reshape(1, n),
        text_lengths.reshape(1, n),
        page_table.reshape(1, n),
        patches,
        vision_gain,
        text_embed,
        attn_gain.reshape(n, 1, width),
        patch_weight,
        merger_inner.T,
        merger_weight,
        q_weight,
        kv_weight.T,
        out_weight,
    )
    return hidden, pool


def solution(mesh):
    in_specs = (
        P("groups"),
        P("groups"),
        P("groups"),
        P(("groups", "wide"), None, None),
        P(),
        P(),
        P(None, "wide"),
        P(None, "wide"),
        P("groups", "wide"),
        P(),
        P(None, "wide"),
        P(None, "wide"),
        P("wide", None),
    )
    out_specs = (P(("groups", "wide"), None), P(("groups", "wide"), None, None, None, None))
    return jax.shard_map(
        on_device, mesh=mesh, in_specs=in_specs, out_specs=out_specs, check_vma=False
    )
```
